32 devices in a mesh: grp: 2 (over y), row: 8 (over z, core), col: 2 (over x).
Axes of the slice: x: 2, y: 2, z: 4, core: 2. Of those that a mesh axis runs over, the one named last changes fastest.
Arguments:
- pair: bfloat16 [192, 96, 128], P(('grp', 'row'), 'col'), parts along dimension 0, may hold values from -6 to 6
- token_count: int32 [2], P('grp'), parts along dimension 0, may hold values from 72 to 96
- tri_in: bfloat16 [2, 128, 512], replicated, may hold values from -0.5 to 0.5
- tri_gate: bfloat16 [2, 128, 128], replicated, may hold values from -0.5 to 0.5
- tri_out: bfloat16 [2, 128, 128], replicated, may hold values from -0.5 to 0.5
- trans_in: bfloat16 [128, 1024], replicated, may hold values from -0.5 to 0.5
- trans_out: bfloat16 [512, 128], replicated, may hold values from -0.25 to 0.25
Outputs:
- pair_out: bfloat16 [192, 96, 128], P(('grp', 'row'), 'col'), parts along dimension 0
The draws below stay inside these ranges and needn't reach their ends.
There are 2 independent parts, one for each index of `grp`. The reference program is written for one: setup_inputs(seed, part) draws one part's arguments, and reference() takes and returns one part's arrays. A program takes and returns all parts, laid end to end along the dimension named above; an argument that names none is the same for every part. Nothing has to cross between parts.
Inputs may be any that keep to these rules, and one draw needn't show every extreme that they name: `token_count`: the number of real tokens of the complex; pair entries with either token index at or past it are padding.
All inputs are finite; a program needn't handle non-finite values.
Results may differ from the reference program's by a relative error of at most 0.015.
Values may be sent and summed in bfloat16 or wider, within the bound.
No kernel may reach another device: no remote copies, remote signals or barrier semaphores. Data moves between devices by JAX's collectives and lax.ppermute only.
A program may use at most 64 MiB of HBM per device.

```python
import jax
import jax.numpy as jnp
from jax import lax

PAIR_DIM = 128
HIDDEN_SIZE = 128
FFN = 512
TOKENS = 96


def levels(own_key, shape, cuts, least, top_value):
    loudness = 1.0
    for position, parts in cuts:
        steps = jax.random.uniform(jax.random.fold_in(jax.random.fold_in(own_key, 6), position), (parts,), jnp.float32, least / len(cuts), top_value / len(cuts))
        loudness = loudness * jnp.repeat(jnp.exp(steps), shape[position] // parts).reshape((-1,) + (1,) * (len(shape) - 1 - position))
    return loudness


def normal_values(rng, extent, width, limit, split=(), held_as=jnp.bfloat16):
    gain = levels(rng, extent, split, -0.22, 0.18) if split else 1.0
    entries = jax.random.normal(rng, extent, jnp.float32) * width * gain
    return jnp.minimum(jnp.maximum(entries, -limit), limit).astype(held_as)


def setup_inputs(seed: int = 0, part: int = 0) -> dict:
    arg_keys = jax.random.split(jax.random.key(seed), 8)
    own_keys = jax.random.split(jax.random.fold_in(arg_keys[7], part), 8)
    pair = normal_values(own_keys[0], (TOKENS, TOKENS, PAIR_DIM), 1.0, 6.0, ((0, 8), (1, 2)))
    token_count = jax.random.randint(own_keys[1], (1,), 3 * TOKENS // 4, TOKENS + 1).astype(jnp.int32)
    tri_in = normal_values(arg_keys[2], (2, PAIR_DIM, 4 * HIDDEN_SIZE), PAIR_DIM ** -0.5, 0.5)
    tri_gate = normal_values(arg_keys[3], (2, PAIR_DIM, PAIR_DIM), PAIR_DIM ** -0.5, 0.5)
    tri_out = normal_values(arg_keys[4], (2, HIDDEN_SIZE, PAIR_DIM), HIDDEN_SIZE ** -0.5, 0.5)
    trans_in = normal_values(arg_keys[5], (PAIR_DIM, 2 * FFN), PAIR_DIM ** -0.5, 0.5)
    trans_out = normal_values(arg_keys[6], (FFN, PAIR_DIM), FFN ** -0.5, 0.25)
    return {"pair": pair, "token_count": token_count, "tri_in": tri_in, "tri_gate": tri_gate, "tri_out": tri_out, "trans_in": trans_in, "trans_out": trans_out}


def layer_norm(values, along):
    average = lax.optimization_barrier(jnp.mean(values, axis=along, keepdims=True))
    centred = values - average
    spread = lax.optimization_barrier(jnp.mean(centred * centred, axis=along, keepdims=True))
    return centred * lax.rsqrt(spread + 1e-05)

def rounded(values):
    return lax.optimization_barrier(values.astype(jnp.bfloat16)).astype(jnp.float32)

def triangle(stream, keep_mask, weight_in, weight_gate, weight_out, from_columns):
    hid_width = weight_out.shape[0]
    normed = rounded(layer_norm(stream.astype(jnp.float32), -1))
    projected = jnp.einsum('ijc,cd->ijd', normed, weight_in.astype(jnp.float32))
    keep_col = keep_mask[:, :, None]
    left_side = rounded(keep_col * jax.nn.sigmoid(projected[..., 2 * hid_width:3 * hid_width]) * projected[..., :hid_width])
    right_side = rounded(keep_col * jax.nn.sigmoid(projected[..., 3 * hid_width:]) * projected[..., hid_width:2 * hid_width])
    gate_value = jax.nn.sigmoid(jnp.einsum('ijc,cd->ijd', normed, weight_gate.astype(jnp.float32)))
    if from_columns:
        mixed_sum = jnp.einsum('kih,kjh->ijh', left_side, right_side)
    else:
        mixed_sum = jnp.einsum('ikh,jkh->ijh', left_side, right_side)
    mix_normed = rounded(layer_norm(mixed_sum, -1))
    update = gate_value * jnp.einsum('ijh,hc->ijc', mix_normed, weight_out.astype(jnp.float32))
    return (stream.astype(jnp.float32) + keep_col * update).astype(jnp.bfloat16)

def reference(pair, token_count, tri_in, tri_gate, tri_out, trans_in, trans_out):
    positions = jnp.arange(TOKENS, dtype=jnp.int32)
    is_valid = (positions < token_count[0]).astype(jnp.float32)
    keep_mask = is_valid[:, None] * is_valid[None, :]
    stream = triangle(pair, keep_mask, tri_in[0], tri_gate[0], tri_out[0], False)
    stream = triangle(stream, keep_mask, tri_in[1], tri_gate[1], tri_out[1], True)
    ffn_width = trans_out.shape[0]
    normed = rounded(layer_norm(stream.astype(jnp.float32), -1))
    inner_sum = jnp.einsum('ijc,cd->ijd', normed, trans_in.astype(jnp.float32))
    activation = rounded(jax.nn.silu(inner_sum[..., :ffn_width]) * inner_sum[..., ffn_width:])
    update = jnp.einsum('ijf,fc->ijc', activation, trans_out.astype(jnp.float32))
    return (stream.astype(jnp.float32) + keep_mask[:, :, None] * update).astype(jnp.bfloat16)
```

```python
import functools

import jax
import jax.numpy as jnp
from jax import lax
from jax.experimental import pallas as pl
from jax.experimental.pallas import tpu as pltpu
from jax.sharding import PartitionSpec as P

F32 = jnp.float32
BF16 = jnp.bfloat16


def norm(values):
    average = jnp.mean(values, axis=-1, keepdims=True)
    centred = values - average
    spread = jnp.mean(centred * centred, axis=-1, keepdims=True)
    return centred * lax.rsqrt(spread + 1e-05)


def dot(left, right):
    return jnp.dot(left, right, preferred_element_type=F32)


def keep_of(place, rows, cols, width):
    shape = (rows, cols, width)
    row = lax.broadcasted_iota(jnp.int32, shape, 0) + place[0]
    col = lax.broadcasted_iota(jnp.int32, shape, 1) + place[1]
    return jnp.where((row < place[2]) & (col < place[2]), 1.0, 0.0).astype(F32)


def gated(normed, weight, which, hidden):
    value = dot(normed, weight[:, which * hidden : (which + 1) * hidden])
    gate = dot(normed, weight[:, (which + 2) * hidden : (which + 3) * hidden])
    return jax.nn.sigmoid(gate) * value


def call(kernel, name, outs, *args, scratch=(), flops=0):
    nbytes = sum(a.size * a.dtype.itemsize for a in (*args[1:], *outs))
    return pl.pallas_call(
        kernel,
        name=name,
        out_shape=outs,
        in_specs=[pl.BlockSpec(memory_space=pltpu.SMEM)]
        + [pl.BlockSpec(memory_space=pltpu.VMEM)] * (len(args) - 1),
        out_specs=[pl.BlockSpec(memory_space=pltpu.VMEM)] * len(outs),
        scratch_shapes=scratch,
        cost_estimate=pl.CostEstimate(flops=flops, bytes_accessed=nbytes, transcendentals=0),
    )(*args)


def start_kernel(place, pair, weight, b_out, normed_out):
    rows, cols, width = pair.shape
    hidden = b_out.shape[2]
    normed = norm(pair[...].astype(F32)).astype(BF16).reshape(rows * cols, width)
    normed_out[...] = normed
    b = gated(normed, weight, 1, hidden).reshape(rows, cols, hidden)
    b_out[...] = (keep_of(place, rows, cols, hidden) * b).astype(BF16)


def second_kernel(place, normed, weight, weight_gate, a_out, gate_out):
    rows, cols, hidden = a_out.shape
    a = gated(normed[...], weight, 0, hidden).reshape(rows, cols, hidden)
    a_out[...] = (keep_of(place, rows, cols, hidden) * a).astype(BF16).astype(F32)
    gate_out[...] = jax.nn.sigmoid(dot(normed[...], weight_gate[...]))


def gate_kernel(place, normed, weight_gate, gate_out):
    gate_out[...] = jax.nn.sigmoid(dot(normed[...], weight_gate[...]))


def mix_rows(place, a, blocks, target, wide):
    rows = a.shape[0]
    step = 2 if rows % 2 == 0 else 1
    for swap, block in enumerate(blocks):
        wide[...] = block[...].astype(F32)
        first = rows * (place[3] ^ swap)

        @pl.loop(0, rows // step)
        def _(turn):
            left = [a[turn * step + s] for s in range(step)]
            for j in range(rows):
                right = wide[j]
                for s in range(step):
                    total = jnp.sum(left[s] * right, axis=0, keepdims=True)
                    target[turn * step + s, pl.ds(first + j, 1), :] = total


def mix_rows_kernel(place, a, b_same, b_other, part_out, wide):
    mix_rows(place, a, (b_same, b_other), part_out, wide)


def mix_rows_last_kernel(parts, place, a, b_same, b_other, *refs):
    earlier, own_out, sends, (part, wide) = (
        refs[: parts - 1],
        refs[parts - 1],
        refs[parts : 2 * parts - 1],
        refs[2 * parts - 1 :],
    )
    mix_rows(place, a, (b_same, b_other), part, wide)
    for group, source in enumerate((*earlier, part)):
        for step in range(parts):

            @pl.when((place[4] ^ step) == group)
            def _():
                if step == 0:
                    own_out[...] = source[...]
                else:
                    sends[step - 1][...] = source[...].astype(BF16).reshape(sends[step - 1].shape)


def middle_kernel(parts, pieces, place, pair, gate, weight_out, weight_in, *refs):
    rows, cols, width = pair.shape
    per = parts
    inputs, (stream_out, a_out, b_out, normed_out), (mixed,) = (
        refs[: per * pieces],
        refs[per * pieces : per * pieces + 4],
        refs[per * pieces + 4 :],
    )
    span = cols // pieces
    for piece in range(pieces):
        own, *others = inputs[piece * per : (piece + 1) * per]
        total = own[...]
        for other in others:
            total = total + other[...].astype(F32).reshape(total.shape)
        slot = place[5] ^ piece
        for where in range(pieces):

            @pl.when(slot == where)
            def _():
                mixed[:, where * span : (where + 1) * span, :] = total

    hidden = mixed.shape[2]
    mixnorm = norm(mixed[...].reshape(rows * cols, hidden)).astype(BF16)
    update = (gate[...] * dot(mixnorm, weight_out[...])).reshape(rows, cols, width)
    keep = keep_of(place, rows, cols, width)
    stream = (pair[...].astype(F32) + keep * update).astype(BF16)
    stream_out[...] = stream
    normed = norm(stream.astype(F32)).astype(BF16).reshape(rows * cols, width)
    normed_out[...] = normed
    a = gated(normed, weight_in, 0, hidden).reshape(rows, cols, hidden)
    a_out[...] = (keep * a).astype(BF16)
    b = gated(normed, weight_in, 1, hidden).reshape(rows, cols, hidden)
    b_out[...] = (keep * b).astype(BF16)


def mix_cols_kernel(parts, group, pieces, place, *refs):
    lefts = refs[: 2 * parts]
    rights = refs[2 * parts : 2 * parts + 2]
    outs = refs[2 * parts + 2 : 2 * parts + 2 + len(pieces)]
    wide_a, wide_b = refs[2 * parts + 2 + len(pieces) :]
    rows, cols, hidden = rights[0].shape
    for step in range(parts):

        @pl.when((place[4] ^ step) == group)
        def _():
            for half in range(2):
                wide_a[half * rows : (half + 1) * rows] = lefts[2 * step + half][...].astype(F32)

    for half in range(2):
        wide_b[half * rows : (half + 1) * rows] = rights[half][...].astype(F32)
    step = 4 if rows % 4 == 0 else 1
    for out, piece in zip(outs, pieces):
        first = ((place[5] ^ piece) * 2 + place[3]) * rows

        @pl.loop(0, rows // step)
        def _(turn):
            totals = [None] * step
            for k in range(2 * rows):
                right = wide_b[k]
                for s in range(step):
                    row = wide_a[k, pl.ds(first + turn * step + s, 1), :]
                    term = row * right
                    totals[s] = term if totals[s] is None else totals[s] + term
            for s in range(step):
                out[turn * step + s] = totals[s].astype(out.dtype)


def last_kernel(place, stream, gate, weight_out, trans_in, trans_out, own, *refs):
    others, (out,) = refs[:-1], refs[-1:]
    rows, cols, width = stream.shape
    total = own[...]
    for other in others:
        total = total + other[...].astype(F32)
    hidden = total.shape[2]
    mixnorm = norm(total.reshape(rows * cols, hidden)).astype(BF16)
    update = (gate[...] * dot(mixnorm, weight_out[...])).reshape(rows, cols, width)
    keep = keep_of(place, rows, cols, width)
    after = (stream[...].astype(F32) + keep * update).astype(BF16)
    normed = norm(after.astype(F32)).astype(BF16).reshape(rows * cols, width)
    ffn = trans_out.shape[0]
    inner = dot(normed, trans_in[:, :ffn])
    act = (jax.nn.silu(inner) * dot(normed, trans_in[:, ffn:])).astype(BF16)
    update = dot(act, trans_out[...]).reshape(rows, cols, width)
    out[...] = (after.astype(F32) + keep * update).astype(BF16)


def body(n_row, n_col, pair, token_count, tri_in, tri_gate, tri_out, trans_in, trans_out):
    rows, cols, width = pair.shape
    hidden = tri_out.shape[1]
    n_chip = n_row // 2
    per = n_chip // n_col
    row_place = lax.axis_index("row")
    col_place = lax.axis_index("col")
    chip = row_place // 2
    lane = jnp.arange(8, dtype=jnp.int32)
    values = (
        row_place * rows,
        col_place * cols,
        token_count[0],
        row_place % 2,
        (chip // per) ^ col_place,
        chip % per,
    )
    place = jnp.zeros((8,), jnp.int32)
    for where, value in enumerate(values):
        place = jnp.where(lane == where, value, place)

    def along_row(value, mask):
        return lax.ppermute(value, "row", [(i, i ^ mask) for i in range(n_row)])

    def along_col(value, mask):
        return lax.ppermute(value, "col", [(i, i ^ mask) for i in range(n_col)])

    def shape(*extent, dtype=BF16):
        return jax.ShapeDtypeStruct(extent, dtype)

    tokens = rows * cols
    b, normed = call(
        start_kernel,
        "start",
        [shape(rows, cols, hidden), shape(tokens, width)],
        place,
        pair,
        tri_in[0],
    )
    arrived = [b] + [along_row(b, 2 * step) for step in range(1, n_chip)]
    a, gate = call(
        second_kernel,
        "second",
        [shape(rows, cols, hidden, dtype=F32), shape(tokens, width, dtype=F32)],
        place,
        normed,
        tri_in[0],
        tri_gate[0],
    )
    blocks = [(block, along_row(block, 1)) for block in arrived]
    wide = pltpu.VMEM((rows, cols, hidden), F32)
    part = shape(rows, 2 * rows, hidden, dtype=F32)
    work = 2 * rows * 2 * rows * cols * hidden
    parts = {}
    inputs = []
    for step in range(n_chip):
        group, piece = divmod(step, per)
        if group < n_col - 1:
            (parts[group, piece],) = call(
                mix_rows_kernel, "mix_rows", [part], place, a, *blocks[step], scratch=[wide], flops=work
            )
        else:
            own, *sends = call(
                functools.partial(mix_rows_last_kernel, n_col),
                "mix_rows_last",
                [part] + [shape(2 * rows * rows, hidden)] * (n_col - 1),
                place,
                a,
                *blocks[step],
                *[parts[other, piece] for other in range(n_col - 1)],
                scratch=[pltpu.VMEM((rows, 2 * rows, hidden), F32), wide],
                flops=work,
            )
            inputs += [own] + [along_col(send, 1 + other) for other, send in enumerate(sends)]
    stream, a, b, normed = call(
        functools.partial(middle_kernel, n_col, per),
        "middle",
        [shape(rows, cols, width), shape(rows, cols, hidden), shape(rows, cols, hidden), shape(tokens, width)],
        place,
        pair,
        gate,
        tri_out[0],
        tri_in[1],
        *inputs,
        scratch=[pltpu.VMEM((rows, cols, hidden), F32)],
    )
    lefts = [a] + [along_col(a, step) for step in range(1, n_col)]
    lefts = [value for left in lefts for value in (left, along_row(left, 1))]
    rights = [b, along_row(b, 1)]
    (gate,) = call(gate_kernel, "gate", [shape(tokens, width, dtype=F32)], place, normed, tri_gate[1])
    totals = {}
    for group in reversed(range(n_col)):
        steps = [group * per + piece for piece in range(per)]
        outs = call(
            functools.partial(mix_cols_kernel, n_col, group, tuple(range(per))),
            "mix_cols",
            [shape(rows, cols, hidden, dtype=BF16 if step else F32) for step in steps],
            place,
            *lefts,
            *rights,
            scratch=[pltpu.VMEM((2 * rows, cols, hidden), F32)] * 2,
            flops=2 * per * rows * cols * 2 * rows * hidden,
        )
        for step, out in zip(steps, outs):
            totals[step] = along_row(out, 2 * step) if step else out
    (out,) = call(
        last_kernel,
        "last",
        [shape(rows, cols, width)],
        place,
        stream,
        gate,
        tri_out[1],
        trans_in,
        trans_out,
        *[totals[step] for step in range(n_chip)],
    )
    return out


def solution(mesh):
    placed = (P(("grp", "row"), "col", None), P("grp"), P(), P(), P(), P(), P())
    return jax.shard_map(
        functools.partial(body, mesh.shape["row"], mesh.shape["col"]),
        mesh=mesh,
        in_specs=placed,
        out_specs=P(("grp", "row"), "col", None),
        check_vma=False,
    )
```

```python
import functools

import jax
import jax.numpy as jnp
from jax import lax
from jax.experimental import pallas as pl
from jax.experimental.pallas import tpu as pltpu
from jax.sharding import PartitionSpec as P

F32 = jnp.float32
VMEM_LIMIT = 24 * 1024 * 1024
BF16 = jnp.bfloat16


def norm(values):
    average = jnp.mean(values, axis=-1, keepdims=True)
    centred = values - average
    spread = jnp.mean(centred * centred, axis=-1, keepdims=True)
    return centred * lax.rsqrt(spread + 1e-05)


def dot(left, right):
    return jnp.dot(left, right, preferred_element_type=F32)


def keep_of(place, rows, cols, width):
    shape = (rows, cols, width)
    row = lax.broadcasted_iota(jnp.int32, shape, 0) + place[0]
    col = lax.broadcasted_iota(jnp.int32, shape, 1) + place[1]
    return jnp.where((row < place[2]) & (col < place[2]), 1.0, 0.0).astype(F32)


def gated(normed, weight, side, which, hidden):
    value = dot(normed, weight[side, :, which * hidden : (which + 1) * hidden])
    gate = dot(normed, weight[side, :, (which + 2) * hidden : (which + 3) * hidden])
    return jax.nn.sigmoid(gate) * value


def call(kernel, name, outs, *args, scratch=(), flops=2_000_000_000):
    nbytes = sum(a.size * a.dtype.itemsize for a in (*args[1:], *outs))
    return pl.pallas_call(
        kernel,
        name=name,
        out_shape=outs,
        in_specs=[pl.BlockSpec(memory_space=pltpu.SMEM)]
        + [pl.BlockSpec(memory_space=pltpu.VMEM)] * (len(args) - 1),
        out_specs=[pl.BlockSpec(memory_space=pltpu.VMEM)] * len(outs),
        scratch_shapes=scratch,
        cost_estimate=pl.CostEstimate(flops=flops, bytes_accessed=nbytes, transcendentals=0),
        compiler_params=pltpu.CompilerParams(vmem_limit_bytes=VMEM_LIMIT),
    )(*args)


def start_kernel(place, pair, weight, b_out, normed_out):
    rows, cols, width = pair.shape
    hidden = b_out.shape[2]
    normed = norm(pair[...].astype(F32)).astype(BF16).reshape(rows * cols, width)
    normed_out[...] = normed
    b = gated(normed, weight, 0, 1, hidden).reshape(rows, cols, hidden)
    b_out[...] = (keep_of(place, rows, cols, hidden) * b).astype(BF16)


def second_kernel(place, normed, weight, weight_gate, a_out, gate_out):
    rows, cols, hidden = a_out.shape
    a = gated(normed[...], weight, 0, 0, hidden).reshape(rows, cols, hidden)
    a_out[...] = (keep_of(place, rows, cols, hidden) * a).astype(BF16).astype(F32)
    gate_out[...] = jax.nn.sigmoid(dot(normed[...], weight_gate[0]))


def gate_kernel(place, normed, weight_gate, gate_out):
    gate_out[...] = jax.nn.sigmoid(dot(normed[...], weight_gate[1]))


def mix_rows(place, a, blocks, target, wide):
    rows = a.shape[0]
    step = 2 if rows % 2 == 0 else 1
    for swap, block in enumerate(blocks):
        wide[...] = block[...].astype(F32)
        first = rows * (place[3] ^ swap)

        @pl.loop(0, rows // step)
        def _(turn):
            left = [a[turn * step + s] for s in range(step)]
            for j in range(rows):
                right = wide[j]
                for s in range(step):
                    total = jnp.sum(left[s] * right, axis=0, keepdims=True)
                    target[turn * step + s, pl.ds(first + j, 1), :] = total


def mix_rows_kernel(place, a, b_same, b_other, part_out, wide):
    mix_rows(place, a, (b_same, b_other), part_out, wide)


def mix_rows_last_kernel(parts, place, a, b_same, b_other, *refs):
    earlier, own_out, sends, (part, wide) = (
        refs[: parts - 1],
        refs[parts - 1],
        refs[parts : 2 * parts - 1],
        refs[2 * parts - 1 :],
    )
    mix_rows(place, a, (b_same, b_other), part, wide)
    for group, source in enumerate((*earlier, part)):
        for step in range(parts):

            @pl.when((place[4] ^ step) == group)
            def _():
                if step == 0:
                    own_out[...] = source[...]
                else:
                    sends[step - 1][...] = source[...].astype(BF16).reshape(sends[step - 1].shape)


def middle_kernel(parts, pieces, place, pair, gate, weight_out, weight_in, *refs):
    rows, cols, width = pair.shape
    per = parts
    inputs, (stream_out, a_out, b_out, normed_out), (mixed,) = (
        refs[: per * pieces],
        refs[per * pieces : per * pieces + 4],
        refs[per * pieces + 4 :],
    )
    span = cols // pieces
    for piece in range(pieces):
        own, *others = inputs[piece * per : (piece + 1) * per]
        total = own[...]
        for other in others:
            total = total + other[...].astype(F32).reshape(total.shape)
        slot = place[5] ^ piece
        for where in range(pieces):

            @pl.when(slot == where)
            def _():
                mixed[:, where * span : (where + 1) * span, :] = total

    hidden = mixed.shape[2]
    mixnorm = norm(mixed[...].reshape(rows * cols, hidden)).astype(BF16)
    update = (gate[...] * dot(mixnorm, weight_out[0])).reshape(rows, cols, width)
    keep = keep_of(place, rows, cols, width)
    stream = (pair[...].astype(F32) + keep * update).astype(BF16)
    stream_out[...] = stream
    normed = norm(stream.astype(F32)).astype(BF16).reshape(rows * cols, width)
    normed_out[...] = normed
    a = gated(normed, weight_in, 1, 0, hidden).reshape(rows, cols, hidden)
    a_out[...] = (keep * a).astype(BF16)
    b = gated(normed, weight_in, 1, 1, hidden).reshape(rows, cols, hidden)
    b_out[...] = (keep * b).astype(BF16)


def mix_cols_kernel(parts, group, pieces, place, *refs):
    lefts = refs[: 2 * parts]
    rights = refs[2 * parts : 2 * parts + 2]
    outs = refs[2 * parts + 2 : 2 * parts + 2 + len(pieces)]
    wide_a, wide_b = refs[2 * parts + 2 + len(pieces) :]
    rows, cols, hidden = rights[0].shape
    for step in range(parts):

        @pl.when((place[4] ^ step) == group)
        def _():
            for half in range(2):
                wide_a[half * rows : (half + 1) * rows] = lefts[2 * step + half][...].astype(F32)

    for half in range(2):
        wide_b[half * rows : (half + 1) * rows] = rights[half][...].astype(F32)
    step = 4 if rows % 4 == 0 else 1
    for out, piece in zip(outs, pieces):
        first = ((place[5] ^ piece) * 2 + place[3]) * rows

        @pl.loop(0, rows // step)
        def _(turn):
            totals = [None] * step
            for k in range(2 * rows):
                right = wide_b[k]
                for s in range(step):
                    row = wide_a[k, pl.ds(first + turn * step + s, 1), :]
                    term = row * right
                    totals[s] = term if totals[s] is None else totals[s] + term
            for s in range(step):
                out[turn * step + s] = totals[s].astype(out.dtype)


def last_kernel(place, stream, gate, weight_out, trans_in, trans_out, own, *refs):
    others, (out,) = refs[:-1], refs[-1:]
    rows, cols, width = stream.shape
    total = own[...]
    for other in others:
        total = total + other[...].astype(F32)
    hidden = total.shape[2]
    mixnorm = norm(total.reshape(rows * cols, hidden)).astype(BF16)
    update = (gate[...] * dot(mixnorm, weight_out[1])).reshape(rows, cols, width)
    keep = keep_of(place, rows, cols, width)
    after = (stream[...].astype(F32) + keep * update).astype(BF16)
    normed = norm(after.astype(F32)).astype(BF16).reshape(rows * cols, width)
    ffn = trans_out.shape[0]
    inner = dot(normed, trans_in[:, :ffn])
    act = (jax.nn.silu(inner) * dot(normed, trans_in[:, ffn:])).astype(BF16)
    update = dot(act, trans_out[...]).reshape(rows, cols, width)
    out[...] = (after.astype(F32) + keep * update).astype(BF16)


def body(n_row, n_col, pair, token_count, tri_in, tri_gate, tri_out, trans_in, trans_out):
    rows, cols, width = pair.shape
    hidden = tri_out.shape[1]
    n_chip = n_row // 2
    per = n_chip // n_col
    row_place = lax.axis_index("row")
    col_place = lax.axis_index("col")
    chip = row_place // 2
    lane = jnp.arange(8, dtype=jnp.int32)
    values = (
        row_place * rows,
        col_place * cols,
        token_count[0],
        row_place % 2,
        (chip // per) ^ col_place,
        chip % per,
    )
    place = jnp.zeros((8,), jnp.int32)
    for where, value in enumerate(values):
        place = jnp.where(lane == where, value, place)

    def along_row(value, mask):
        return lax.ppermute(value, "row", [(i, i ^ mask) for i in range(n_row)])

    def along_col(value, mask):
        return lax.ppermute(value, "col", [(i, i ^ mask) for i in range(n_col)])

    def shape(*extent, dtype=BF16):
        return jax.ShapeDtypeStruct(extent, dtype)

    tokens = rows * cols
    b, normed = call(
        start_kernel,
        "start",
        [shape(rows, cols, hidden), shape(tokens, width)],
        place,
        pair,
        tri_in,
    )
    arrived = [b] + [along_row(b, 2 * step) for step in range(1, n_chip)]
    a, gate = call(
        second_kernel,
        "second",
        [shape(rows, cols, hidden, dtype=F32), shape(tokens, width, dtype=F32)],
        place,
        normed,
        tri_in,
        tri_gate,
    )
    blocks = [(block, along_row(block, 1)) for block in arrived]
    wide = pltpu.VMEM((rows, cols, hidden), F32)
    part = shape(rows, 2 * rows, hidden, dtype=F32)
    parts = {}
    inputs = []
    for step in range(n_chip):
        group, piece = divmod(step, per)
        if group < n_col - 1:
            (parts[group, piece],) = call(
                mix_rows_kernel, "mix_rows", [part], place, a, *blocks[step], scratch=[wide]
            )
        else:
            own, *sends = call(
                functools.partial(mix_rows_last_kernel, n_col),
                "mix_rows_last",
                [part] + [shape(2 * rows * rows, hidden)] * (n_col - 1),
                place,
                a,
                *blocks[step],
                *[parts[other, piece] for other in range(n_col - 1)],
                scratch=[pltpu.VMEM((rows, 2 * rows, hidden), F32), wide],
            )
            inputs += [own] + [along_col(send, 1 + other) for other, send in enumerate(sends)]
    stream, a, b, normed = call(
        functools.partial(middle_kernel, n_col, per),
        "middle",
        [shape(rows, cols, width), shape(rows, cols, hidden), shape(rows, cols, hidden), shape(tokens, width)],
        place,
        pair,
        gate,
        tri_out,
        tri_in,
        *inputs,
        scratch=[pltpu.VMEM((rows, cols, hidden), F32)],
    )
    lefts = [a] + [along_col(a, step) for step in range(1, n_col)]
    lefts = [value for left in lefts for value in (left, along_row(left, 1))]
    rights = [b, along_row(b, 1)]
    (gate,) = call(gate_kernel, "gate", [shape(tokens, width, dtype=F32)], place, normed, tri_gate)
    totals = {}
    for group in reversed(range(n_col)):
        steps = [group * per + piece for piece in range(per)]
        outs = call(
            functools.partial(mix_cols_kernel, n_col, group, tuple(range(per))),
            "mix_cols",
            [shape(rows, cols, hidden, dtype=BF16 if step else F32) for step in steps],
            place,
            *lefts,
            *rights,
            scratch=[pltpu.VMEM((2 * rows, cols, hidden), F32)] * 2,
        )
        for step, out in zip(steps, outs):
            totals[step] = along_row(out, 2 * step) if step else out
    (out,) = call(
        last_kernel,
        "last",
        [shape(rows, cols, width)],
        place,
        stream,
        gate,
        tri_out,
        trans_in,
        trans_out,
        *[totals[step] for step in range(n_chip)],
    )
    return out


def solution(mesh):
    placed = (P(("grp", "row"), "col", None), P("grp"), P(), P(), P(), P(), P())
    return jax.shard_map(
        functools.partial(body, mesh.shape["row"], mesh.shape["col"]),
        mesh=mesh,
        in_specs=placed,
        out_specs=P(("grp", "row"), "col", None),
        check_vma=False,
    )
```

```python
import functools

import jax
import jax.numpy as jnp
from jax import lax
from jax.experimental import pallas as pl
from jax.experimental.pallas import tpu as pltpu
from jax.sharding import PartitionSpec as P


F32 = jnp.float32
VMEM_LIMIT = 24 * 1024 * 1024
BF16 = jnp.bfloat16


def norm(values):
    average = jnp.mean(values, axis=-1, keepdims=True)
    centred = values - average
    spread = jnp.mean(centred * centred, axis=-1, keepdims=True)
    return centred * lax.rsqrt(spread + 1e-05)


def dot(left, right):
    return jnp.dot(left, right, preferred_element_type=F32)


def keep_of(place, rows, cols, width):
    shape = (rows, cols, width)
    row = lax.broadcasted_iota(jnp.int32, shape, 0) + place[0]
    col = lax.broadcasted_iota(jnp.int32, shape, 1) + place[1]
    return jnp.where((row < place[2]) & (col < place[2]), 1.0, 0.0).astype(F32)


def gated(normed, weight, side, which, hidden):
    value = dot(normed, weight[side, :, which * hidden : (which + 1) * hidden])
    gate = dot(normed, weight[side, :, (which + 2) * hidden : (which + 3) * hidden])
    return jax.nn.sigmoid(gate) * value


def call(kernel, outs, *args, scratch=(), flops=2_000_000_000, space=pltpu.VMEM):
    nbytes = sum(a.size * a.dtype.itemsize for a in (*args[1:], *outs))
    return pl.pallas_call(
        kernel,
        out_shape=outs,
        in_specs=[pl.BlockSpec(memory_space=pltpu.SMEM)]
        + [pl.BlockSpec(memory_space=space)] * (len(args) - 1),
        out_specs=[pl.BlockSpec(memory_space=pltpu.VMEM)] * len(outs),
        scratch_shapes=scratch,
        cost_estimate=pl.CostEstimate(flops=flops, bytes_accessed=nbytes, transcendentals=0),
        compiler_params=pltpu.CompilerParams(vmem_limit_bytes=VMEM_LIMIT),
    )(*args)


def start_kernel(place, pair, weight, b_out, tile, value, gate, sems):
    rows, cols, width = pair.shape
    hidden = b_out.shape[2]
    copies = [
        pltpu.make_async_copy(source, target, sems.at[turn])
        for turn, (source, target) in enumerate(
            (
                (pair, tile),
                (weight.at[0, :, hidden : 2 * hidden], value),
                (weight.at[0, :, 3 * hidden :], gate),
            )
        )
    ]
    for copy in copies:
        copy.start()
    for copy in copies:
        copy.wait()
    normed = norm(tile[...].astype(F32)).astype(BF16).reshape(rows * cols, width)
    b = (jax.nn.sigmoid(dot(normed, gate[...])) * dot(normed, value[...])).reshape(rows, cols, hidden)
    b_out[...] = (keep_of(place, rows, cols, hidden) * b).astype(BF16)


def second_kernel(place, pair, weight, a_out):
    rows, cols, width = pair.shape
    hidden = a_out.shape[2]
    normed = norm(pair[...].astype(F32)).astype(BF16).reshape(rows * cols, width)
    a = gated(normed, weight, 0, 0, hidden).reshape(rows, cols, hidden)
    a_out[...] = (keep_of(place, rows, cols, hidden) * a).astype(BF16).astype(F32)


def gates_kernel(place, weight_gate, *refs):
    *tiles, pairs_out, gates_out = refs
    rows, cols, width = tiles[0].shape
    span = 2 * rows
    per = cols // span
    for step, tile in enumerate(tiles):
        wide = tile[...].astype(F32)
        for piece in range(per):
            cut = wide[:, piece * span : (piece + 1) * span, :].reshape(rows * span, width)
            pairs_out[step * per + piece] = cut
            gates_out[step * per + piece] = jax.nn.sigmoid(dot(norm(cut).astype(BF16), weight_gate[0]))


def mix_rows_kernel(send, place, a, b_same, b_other, *refs):
    earlier, (part_out, *send_out), wide = (refs[: max(send - 1, 0)], refs[max(send - 1, 0) : -1], refs[-1])
    rows = a.shape[0]
    step = 2 if rows % 2 == 0 else 1
    for swap, block in enumerate((b_same, b_other)):
        wide[...] = block[...].astype(F32)
        first = rows * (place[3] ^ swap)

        @pl.loop(0, rows // step)
        def _(turn):
            left = [a[turn * step + s] for s in range(step)]
            for j in range(rows):
                right = wide[j]
                for s in range(step):
                    total = jnp.sum(left[s] * right, axis=0, keepdims=True)
                    part_out[turn * step + s, pl.ds(first + j, 1), :] = total

    cut = part_out.shape[0] * part_out.shape[1]
    for turn, part in enumerate((*earlier, part_out) if send else ()):
        send_out[0][turn * cut : (turn + 1) * cut] = part[...].reshape(cut, part.shape[2]).astype(BF16)


def middle_kernel(step, per, which_cut, place, pairs, gates, weight_out, weight_in, part, *refs):
    *others, stream_out, ab_out = refs
    rows, span, hidden = part.shape
    width = pairs.shape[2]
    total = part[...].reshape(rows * span, hidden)
    for other in others:
        total = total + other[which_cut * rows * span : (which_cut + 1) * rows * span].astype(F32)
    group, piece = divmod(step, per)
    which = (place[4] ^ group) * per + (place[5] ^ piece)
    mixnorm = norm(total).astype(BF16)
    update = gates[which] * dot(mixnorm, weight_out[0])
    shape = (rows, span, width)
    row = lax.broadcasted_iota(jnp.int32, shape, 0) + place[0]
    col = lax.broadcasted_iota(jnp.int32, shape, 1) + (place[6] ^ step) * span
    keep = jnp.where((row < place[2]) & (col < place[2]), 1.0, 0.0).astype(F32).reshape(rows * span, width)
    stream = (pairs[which] + keep * update).astype(BF16)
    stream_out[...] = stream
    normed = norm(stream.astype(F32)).astype(BF16)
    for side in range(2):
        value = keep * gated(normed, weight_in, 1, side, hidden)
        ab_out[side] = value.reshape(rows, span, hidden).astype(BF16)


def mix_cols_kernel(per, step, place, *refs):
    same, other = refs[: (len(refs) - 3) // 2], refs[(len(refs) - 3) // 2 : -3]
    out, wide_a, wide_b = refs[-3:]
    _, rows, span, _ = same[0].shape
    for half, source in enumerate((same[step], other[step])):
        wide_a[half * rows : (half + 1) * rows] = source[0].astype(F32)
    for group in range(len(same) // per):

        @pl.when(place[4] == group)
        def _():
            for piece in range(per):
                first = pl.multiple_of((place[5] ^ piece) * span, 8)
                for half, source in enumerate((same, other)):
                    value = source[group * per + piece][1].astype(F32)
                    wide_b[half * rows : (half + 1) * rows, pl.ds(first, span), :] = value

    steps = 4 if rows % 4 == 0 else 1
    first = place[3] * rows

    @pl.loop(0, rows // steps)
    def _(turn):
        totals = [None] * steps
        for k in range(2 * rows):
            right = wide_b[k]
            for s in range(steps):
                row = wide_a[k, pl.ds(first + turn * steps + s, 1), :]
                term = row * right
                totals[s] = term if totals[s] is None else totals[s] + term
        for s in range(steps):
            out[turn * steps + s] = totals[s].astype(out.dtype)


def own_kernel(per, place, weight_gate, *refs):
    *pieces, stream_out, gate_out, wide = refs
    rows, cols, width = stream_out.shape
    span = 2 * rows
    for group in range(len(pieces) // per):

        @pl.when(place[4] == group)
        def _():
            for piece in range(per):
                first = pl.multiple_of((place[5] ^ piece) * span, 8)
                value = pieces[group * per + piece][...].astype(F32).reshape(rows, span, width)
                wide[:, pl.ds(first, span), :] = value

    stream = wide[...]
    stream_out[...] = stream.astype(BF16)
    normed = norm(stream).astype(BF16).reshape(rows * cols, width)
    gate_out[...] = jax.nn.sigmoid(dot(normed, weight_gate[1]))


def last_kernel(place, stream, gate, weight_out, trans_in, trans_out, own, *refs):
    others, (out,) = refs[:-1], refs[-1:]
    rows, cols, width = stream.shape
    total = own[...]
    for other in others:
        total = total + other[...].astype(F32)
    hidden = total.shape[2]
    mixnorm = norm(total.reshape(rows * cols, hidden)).astype(BF16)
    update = (gate[...] * dot(mixnorm, weight_out[1])).reshape(rows, cols, width)
    keep = keep_of(place, rows, cols, width)
    after = (stream[...].astype(F32) + keep * update).astype(BF16)
    normed = norm(after.astype(F32)).astype(BF16).reshape(rows * cols, width)
    ffn = trans_out.shape[0]
    inner = dot(normed, trans_in[:, :ffn])
    act = (jax.nn.silu(inner) * dot(normed, trans_in[:, ffn:])).astype(BF16)
    update = dot(act, trans_out[...]).reshape(rows, cols, width)
    out[...] = (after.astype(F32) + keep * update).astype(BF16)


def sequence(n_chip):
    return [0, 1, *range(n_chip - 1, 1, -1)]


def sending(n_chip):
    return [*range(min(2, n_chip - 1), n_chip), *range(min(2, n_chip - 1) - 1, -1, -1)]


def body(n_row, n_col, pair, token_count, tri_in, tri_gate, tri_out, trans_in, trans_out):
    rows, cols, width = pair.shape
    hidden = tri_out.shape[1]
    n_chip = n_row // 2
    per = n_chip // n_col
    span = 2 * rows
    row_place = lax.axis_index("row")
    col_place = lax.axis_index("col")
    chip = row_place // 2
    lane = jnp.arange(8, dtype=jnp.int32)
    values = (
        row_place * rows,
        col_place * cols,
        token_count[0],
        row_place % 2,
        (chip // per) ^ col_place,
        chip % per,
        chip,
    )
    place = jnp.zeros((8,), jnp.int32)
    for where, value in enumerate(values):
        place = jnp.where(lane == where, value, place)

    def along_row(value, mask):
        return lax.ppermute(value, "row", [(i, i ^ mask) for i in range(n_row)])

    def along_col(value, mask):
        return lax.ppermute(value, "col", [(i, i ^ mask) for i in range(n_col)])

    def shape(*extent, dtype=BF16):
        return jax.ShapeDtypeStruct(extent, dtype)

    tile = (rows, cols, hidden)
    cut = (rows * span, width)
    tiles = [pair] + [along_col(pair, step) for step in range(1, n_col)]
    (b,) = call(
        start_kernel,
        [shape(*tile)],
        place,
        pltpu.with_memory_space_constraint(pair, pltpu.HBM),
        pltpu.with_memory_space_constraint(tri_in, pltpu.HBM),
        scratch=[
            pltpu.VMEM((rows, cols, width), BF16),
            pltpu.VMEM((width, hidden), BF16),
            pltpu.VMEM((width, hidden), BF16),
            pltpu.SemaphoreType.DMA((3,)),
        ],
        space=pltpu.HBM,
    )
    turns = sequence(n_chip)
    arrived = {0: b}
    for step in turns[1:]:
        arrived[step] = along_row(b, 2 * step)
    (a,) = call(second_kernel, [shape(*tile, dtype=F32)], place, pair, tri_in)
    pairs, gates = call(gates_kernel, [shape(n_chip, *cut, dtype=F32)] * 2, place, tri_gate, *tiles)
    streams, same, other = ({}, {}, {})
    parts = {}
    joined = turns[:2]
    for step in turns:
        block = arrived[step]
        send = {joined[0]: 0, joined[1]: 2}.get(step, 1)
        parts[step], *sent = call(
            functools.partial(mix_rows_kernel, send),
            [shape(rows, span, hidden, dtype=F32)] + [shape(send * rows * span, hidden)] * (send > 0),
            place,
            a,
            block,
            along_row(block, 1),
            *[parts[before] for before in joined[:1] if send > 1],
            scratch=[pltpu.VMEM(tile, F32)],
        )
        if not send:
            continue
        sent = [along_col(sent[0], mask) for mask in range(1, n_col)]
        for which, ready in enumerate(joined if send > 1 else [step]):
            streams[ready], same[ready] = call(
                functools.partial(middle_kernel, ready, per, which),
                [shape(*cut), shape(2, rows, span, hidden)],
                place,
                pairs,
                gates,
                tri_out,
                tri_in,
                parts[ready],
                *sent,
            )
            other[ready] = along_row(same[ready], 1)
    totals = {}
    streams, same, other = ([values[step] for step in range(n_chip)] for values in (streams, same, other))
    for step in sending(n_chip):
        (out,) = call(
            functools.partial(mix_cols_kernel, per, step),
            [shape(*tile, dtype=BF16 if step else F32)],
            place,
            *same,
            *other,
            scratch=[pltpu.VMEM((span, span, hidden), F32), pltpu.VMEM((span, cols, hidden), F32)],
        )
        totals[step] = along_row(out, 2 * step) if step else out
    stream, gate = call(
        functools.partial(own_kernel, per),
        [shape(rows, cols, width), shape(rows * cols, width, dtype=F32)],
        place,
        tri_gate,
        *streams,
        scratch=[pltpu.VMEM((rows, cols, width), F32)],
    )
    (out,) = call(
        last_kernel,
        [shape(rows, cols, width)],
        place,
        stream,
        gate,
        tri_out,
        trans_in,
        trans_out,
        *[totals[step] for step in range(n_chip)],
    )
    return out


def solution(mesh):
    placed = (P(("grp", "row"), "col", None), P("grp"), P(), P(), P(), P(), P())

    def step(*args):
        return body(mesh.shape["row"], mesh.shape["col"], *args)

    return jax.shard_map(
        step,
        mesh=mesh,
        in_specs=placed,
        out_specs=P(("grp", "row"), "col", None),
        check_vma=False,
    )
```

```python
import functools

import jax
import jax.numpy as jnp
from jax import lax
from jax.experimental import pallas as pl
from jax.experimental.pallas import tpu as pltpu
from jax.sharding import PartitionSpec as P


F32 = jnp.float32
VMEM_LIMIT = 24 * 1024 * 1024
BF16 = jnp.bfloat16


def norm(values):
    average = jnp.mean(values, axis=-1, keepdims=True)
    centred = values - average
    spread = jnp.mean(centred * centred, axis=-1, keepdims=True)
    return centred * lax.rsqrt(spread + 1e-05)


def dot(left, right):
    return jnp.dot(left, right, preferred_element_type=F32)


class Place:

    def __init__(self, n_row, n_col, limit=None):
        self.n_row, self.n_col, self.limit = n_row, n_col, limit
        self.per = n_row // 2 // n_col

    def row(self):
        return lax.axis_index("row")

    def col(self):
        return lax.axis_index("col")

    def core(self):
        return lax.rem(self.row(), 2)

    def chip(self):
        return lax.div(self.row(), 2)

    def group(self):
        return lax.div(self.chip(), self.per) ^ self.col()

    def piece(self):
        return lax.rem(self.chip(), self.per)

    def keep(self, first_row, first_col, shape):
        row = lax.broadcasted_iota(jnp.int32, shape, 0) + first_row
        col = lax.broadcasted_iota(jnp.int32, shape, 1) + first_col
        count = self.limit[:1, : shape[2]].reshape(1, 1, shape[2])
        return jnp.where((row < count) & (col < count), 1.0, 0.0).astype(F32)


def gated(normed, weight, side, which, hidden):
    value = dot(normed, weight[side, :, which * hidden : (which + 1) * hidden])
    gate = dot(normed, weight[side, :, (which + 2) * hidden : (which + 3) * hidden])
    return jax.nn.sigmoid(gate) * value


def call(kernel, outs, place, *args, scratch=(), flops=2_000_000_000, space=pltpu.VMEM, masked=False):
    nbytes = sum(a.size * a.dtype.itemsize for a in (*args, *outs))

    def run(*refs):
        if masked:
            kernel(Place(place.n_row, place.n_col, refs[0]), *refs[1:])
        else:
            kernel(place, *refs)

    limit = [place.limit] if masked else []
    run = pl.pallas_call(
        run,
        out_shape=outs,
        in_specs=[pl.BlockSpec(memory_space=pltpu.VMEM)] * len(limit)
        + [pl.BlockSpec(memory_space=space)] * len(args),
        out_specs=[pl.BlockSpec(memory_space=pltpu.VMEM)] * len(outs),
        scratch_shapes=scratch,
        cost_estimate=pl.CostEstimate(flops=flops, bytes_accessed=nbytes, transcendentals=0),
        compiler_params=pltpu.CompilerParams(vmem_limit_bytes=VMEM_LIMIT),
    )
    return run(*limit, *args)


def start_kernel(place, pair, weight, b_out, tile, value, gate, sems):
    rows, cols, width = pair.shape
    hidden = b_out.shape[2]
    copies = [
        pltpu.make_async_copy(source, target, sems.at[turn])
        for turn, (source, target) in enumerate(
            (
                (pair, tile),
                (weight.at[0, :, hidden : 2 * hidden], value),
                (weight.at[0, :, 3 * hidden :], gate),
            )
        )
    ]
    for copy in copies:
        copy.start()
    for copy in copies:
        copy.wait()
    normed = norm(tile[...].astype(F32)).astype(BF16).reshape(rows * cols, width)
    b = (jax.nn.sigmoid(dot(normed, gate[...])) * dot(normed, value[...])).reshape(rows, cols, hidden)
    b_out[...] = (place.keep(place.row() * rows, place.col() * cols, (rows, cols, hidden)) * b).astype(BF16)


def second_kernel(place, pair, weight, a_out):
    rows, cols, width = pair.shape
    hidden = a_out.shape[2]
    normed = norm(pair[...].astype(F32)).astype(BF16).reshape(rows * cols, width)
    a = gated(normed, weight, 0, 0, hidden).reshape(rows, cols, hidden)
    a_out[...] = (place.keep(place.row() * rows, place.col() * cols, (rows, cols, hidden)) * a).astype(BF16).astype(F32)


def gates_kernel(place, weight_gate, *refs):
    *tiles, pairs_out, gates_out = refs
    rows, cols, width = tiles[0].shape
    span = 2 * rows
    per = cols // span
    for step, tile in enumerate(tiles):
        wide = tile[...].astype(F32)
        for piece in range(per):
            cut = wide[:, piece * span : (piece + 1) * span, :].reshape(rows * span, width)
            pairs_out[step * per + piece] = cut
            gates_out[step * per + piece] = jax.nn.sigmoid(dot(norm(cut).astype(BF16), weight_gate[0]))


def mix_rows_kernel(send, place, a, b_same, b_other, *refs):
    earlier, (part_out, *send_out), wide = (refs[: max(send - 1, 0)], refs[max(send - 1, 0) : -1], refs[-1])
    rows = a.shape[0]
    step = 2 if rows % 2 == 0 else 1
    for swap, block in enumerate((b_same, b_other)):
        wide[...] = block[...].astype(F32)
        first = rows * (place.core() ^ swap)

        @pl.loop(0, rows // step)
        def _(turn):
            left = [a[turn * step + s] for s in range(step)]
            for j in range(rows):
                right = wide[j]
                for s in range(step):
                    total = jnp.sum(left[s] * right, axis=0, keepdims=True)
                    part_out[turn * step + s, pl.ds(first + j, 1), :] = total

    cut = part_out.shape[0] * part_out.shape[1]
    for turn, part in enumerate((*earlier, part_out) if send else ()):
        send_out[0][turn * cut : (turn + 1) * cut] = part[...].reshape(cut, part.shape[2]).astype(BF16)


def middle_kernel(step, per, which_cut, place, pairs, gates, weight_out, weight_in, part, *refs):
    *others, stream_out, ab_out = refs
    rows, span, hidden = part.shape
    width = pairs.shape[2]
    total = part[...].reshape(rows * span, hidden)
    for other in others:
        total = total + other[which_cut * rows * span : (which_cut + 1) * rows * span].astype(F32)
    group, piece = divmod(step, per)
    which = (place.group() ^ group) * per + (place.piece() ^ piece)
    mixnorm = norm(total).astype(BF16)
    update = gates[which] * dot(mixnorm, weight_out[0])
    shape = (rows, span, width)
    keep = place.keep(place.row() * rows, (place.chip() ^ step) * span, shape).reshape(rows * span, width)
    stream = (pairs[which] + keep * update).astype(BF16)
    stream_out[...] = stream
    normed = norm(stream.astype(F32)).astype(BF16)
    for side in range(2):
        value = keep * gated(normed, weight_in, 1, side, hidden)
        ab_out[side] = value.reshape(rows, span, hidden).astype(BF16)


def mix_cols_kernel(per, step, place, *refs):
    same, other = refs[: (len(refs) - 3) // 2], refs[(len(refs) - 3) // 2 : -3]
    out, wide_a, wide_b = refs[-3:]
    _, rows, span, _ = same[0].shape
    for half, source in enumerate((same[step], other[step])):
        wide_a[half * rows : (half + 1) * rows] = source[0].astype(F32)
    for group in range(len(same) // per):

        @pl.when(place.group() == group)
        def _():
            for piece in range(per):
                first = pl.multiple_of((place.piece() ^ piece) * span, 8)
                for half, source in enumerate((same, other)):
                    value = source[group * per + piece][1].astype(F32)
                    wide_b[half * rows : (half + 1) * rows, pl.ds(first, span), :] = value

    steps = 4 if rows % 4 == 0 else 1
    first = place.core() * rows

    @pl.loop(0, rows // steps)
    def _(turn):
        totals = [None] * steps
        for k in range(2 * rows):
            right = wide_b[k]
            for s in range(steps):
                row = wide_a[k, pl.ds(first + turn * steps + s, 1), :]
                term = row * right
                totals[s] = term if totals[s] is None else totals[s] + term
        for s in range(steps):
            out[turn * steps + s] = totals[s].astype(out.dtype)


def own_kernel(per, place, weight_gate, *refs):
    *pieces, stream_out, gate_out, wide = refs
    rows, cols, width = stream_out.shape
    span = 2 * rows
    for group in range(len(pieces) // per):

        @pl.when(place.group() == group)
        def _():
            for piece in range(per):
                first = pl.multiple_of((place.piece() ^ piece) * span, 8)
                value = pieces[group * per + piece][...].astype(F32).reshape(rows, span, width)
                wide[:, pl.ds(first, span), :] = value

    stream = wide[...]
    stream_out[...] = stream.astype(BF16)
    normed = norm(stream).astype(BF16).reshape(rows * cols, width)
    gate_out[...] = jax.nn.sigmoid(dot(normed, weight_gate[1]))


def last_kernel(place, stream, gate, weight_out, trans_in, trans_out, own, *refs):
    others, (out,) = refs[:-1], refs[-1:]
    rows, cols, width = stream.shape
    total = own[...]
    for other in others:
        total = total + other[...].astype(F32)
    hidden = total.shape[2]
    mixnorm = norm(total.reshape(rows * cols, hidden)).astype(BF16)
    update = (gate[...] * dot(mixnorm, weight_out[1])).reshape(rows, cols, width)
    keep = place.keep(place.row() * rows, place.col() * cols, (rows, cols, width))
    after = (stream[...].astype(F32) + keep * update).astype(BF16)
    normed = norm(after.astype(F32)).astype(BF16).reshape(rows * cols, width)
    ffn = trans_out.shape[0]
    inner = dot(normed, trans_in[:, :ffn])
    act = (jax.nn.silu(inner) * dot(normed, trans_in[:, ffn:])).astype(BF16)
    update = dot(act, trans_out[...]).reshape(rows, cols, width)
    out[...] = (after.astype(F32) + keep * update).astype(BF16)


def sequence(n_chip):
    return [0, 1, *range(n_chip - 1, 1, -1)]


def sending(n_chip):
    return [*range(min(2, n_chip - 1), n_chip), *range(min(2, n_chip - 1) - 1, -1, -1)]


def body(n_row, n_col, pair, token_count, tri_in, tri_gate, tri_out, trans_in, trans_out):
    rows, cols, width = pair.shape
    hidden = tri_out.shape[1]
    n_chip = n_row // 2
    per = n_chip // n_col
    span = 2 * rows
    limit = jnp.broadcast_to(token_count.reshape(1, 1), (8, max(width, hidden)))
    place = Place(n_row, n_col, limit)

    def along_row(value, mask):
        return lax.ppermute(value, "row", [(i, i ^ mask) for i in range(n_row)])

    def along_col(value, mask):
        return lax.ppermute(value, "col", [(i, i ^ mask) for i in range(n_col)])

    def shape(*extent, dtype=BF16):
        return jax.ShapeDtypeStruct(extent, dtype)

    tile = (rows, cols, hidden)
    cut = (rows * span, width)
    tiles = [pair] + [along_col(pair, step) for step in range(1, n_col)]
    (b,) = call(
        start_kernel,
        [shape(*tile)],
        place,
        pltpu.with_memory_space_constraint(pair, pltpu.HBM),
        pltpu.with_memory_space_constraint(tri_in, pltpu.HBM),
        scratch=[
            pltpu.VMEM((rows, cols, width), BF16),
            pltpu.VMEM((width, hidden), BF16),
            pltpu.VMEM((width, hidden), BF16),
            pltpu.SemaphoreType.DMA((3,)),
        ],
        space=pltpu.HBM,
        masked=True,
    )
    turns = sequence(n_chip)
    arrived = {0: b}
    for step in turns[1:]:
        arrived[step] = along_row(b, 2 * step)
    (a,) = call(second_kernel, [shape(*tile, dtype=F32)], place, pair, tri_in, masked=True)
    pairs, gates = call(gates_kernel, [shape(n_chip, *cut, dtype=F32)] * 2, place, tri_gate, *tiles)
    streams, same, other = ({}, {}, {})
    parts = {}
    joined = turns[:2]
    for step in turns:
        block = arrived[step]
        send = {joined[0]: 0, joined[1]: 2}.get(step, 1)
        parts[step], *sent = call(
            functools.partial(mix_rows_kernel, send),
            [shape(rows, span, hidden, dtype=F32)] + [shape(send * rows * span, hidden)] * (send > 0),
            place,
            a,
            block,
            along_row(block, 1),
            *[parts[before] for before in joined[:1] if send > 1],
            scratch=[pltpu.VMEM(tile, F32)],
        )
        if not send:
            continue
        sent = [along_col(sent[0], mask) for mask in range(1, n_col)]
        for which, ready in enumerate(joined if send > 1 else [step]):
            streams[ready], same[ready] = call(
                functools.partial(middle_kernel, ready, per, which),
                [shape(*cut), shape(2, rows, span, hidden)],
                place,
                pairs,
                gates,
                tri_out,
                tri_in,
                parts[ready],
                *sent,
                masked=True,
            )
            other[ready] = along_row(same[ready], 1)
    totals = {}
    streams, same, other = ([values[step] for step in range(n_chip)] for values in (streams, same, other))
    for step in sending(n_chip):
        (out,) = call(
            functools.partial(mix_cols_kernel, per, step),
            [shape(*tile, dtype=BF16 if step else F32)],
            place,
            *same,
            *other,
            scratch=[pltpu.VMEM((span, span, hidden), F32), pltpu.VMEM((span, cols, hidden), F32)],
        )
        totals[step] = along_row(out, 2 * step) if step else out
    stream, gate = call(
        functools.partial(own_kernel, per),
        [shape(rows, cols, width), shape(rows * cols, width, dtype=F32)],
        place,
        tri_gate,
        *streams,
        scratch=[pltpu.VMEM((rows, cols, width), F32)],
    )
    (out,) = call(
        last_kernel,
        [shape(rows, cols, width)],
        place,
        stream,
        gate,
        tri_out,
        trans_in,
        trans_out,
        *[totals[step] for step in range(n_chip)],
        masked=True,
    )
    return out


def solution(mesh):
    placed = (P(("grp", "row"), "col", None), P("grp"), P(), P(), P(), P(), P())

    def step(*args):
        return body(mesh.shape["row"], mesh.shape["col"], *args)

    return jax.shard_map(
        step,
        mesh=mesh,
        in_specs=placed,
        out_specs=P(("grp", "row"), "col", None),
        check_vma=False,
    )
```
